256 devices in a mesh: ctx: 32 (over z, x), exp: 8 (over y, core).
Axes of the slice: x: 4, y: 4, z: 8, core: 2. Of those that a mesh axis runs over, the one named last changes fastest.
Arguments:
- grad_out: bfloat16 [32768, 2880], P(('ctx', 'exp')), may hold values from -6 to 6
- top_logits: float32 [32768, 4], P(('ctx', 'exp')), may hold values from -8 to 308
- expert_ids: int32 [32768, 4], P(('ctx', 'exp')), may hold values from 0 to 7, all different within a row; in each aligned block of 128 rows (0 to 127, 128 to 255, ...) at most 96 rows name the same one
- saved_hidden: bfloat16 [32, 8, 768, 1536], P('ctx', 'exp'), may hold values from -0.29882812 to 0.29882812
- w_down: bfloat16 [8, 1536, 2880], P('exp', 'ctx'), may hold values from -0.15625 to 0.15625
Outputs:
- logit_grad: float32 [32768, 4], P(('ctx', 'exp'))
- hidden_grad: bfloat16 [32, 8, 768, 1536], P('ctx', 'exp')
- down_grad: float32 [8, 1536, 2880], P('exp', 'ctx')
The draws below stay inside these ranges and needn't reach their ends.
Inputs may be any that keep to these rules, and one draw needn't show every extreme that they name: `expert_ids`: each row names 4 different experts; among the rows of one device no expert is named by more than 96 rows, a bound that some blocks reach.
All inputs are finite; a program needn't handle non-finite values.
Results may differ from the reference program's by a relative error of at most 0.0048.
Values may be sent and summed in bfloat16 or wider, within the bound.
A program may use at most 128 MiB of HBM per device.

```python
import math
import jax
import jax.numpy as jnp
import numpy as np
from jax import lax

D = 2880
TOPK = 4
FF = 1536
TOK_DEV = 128
EXPERTS = 8
CAP = 96
SLOTS = 768
TOKENS = 32768
N_CTX = 32
N_EXP = 8


def draw_top_logits(key, part):
    base_key = jax.random.fold_in(jax.random.fold_in(key, 7), 0)
    values = jnp.clip(1.5 * jax.random.normal(base_key, (TOKENS, TOPK), jnp.float32), -8.0, 8.0)
    return values


def level_of(stream_key, extent, cuts, smallest, largest):
    def one(position, blocks):
        steps = jax.random.uniform(jax.random.fold_in(jax.random.fold_in(stream_key, 6), position), (blocks,), jnp.float32, smallest / len(cuts), largest / len(cuts))
        return jnp.repeat(jnp.exp(steps), extent[position] // blocks).reshape((-1,) + (1,) * (len(extent) - position - 1))

    loudness = one(*cuts[0])
    for cut in cuts[1:]:
        loudness = loudness * one(*cut)
    return loudness


def shared_out(stream_key, own, number, rows, number_of, top, most, skew):
    sequence = jax.random.permutation(stream_key, number_of)
    packed, ordinary = portions_of(number_of, rows * top, most, skew, True), portions_of(number_of, rows * top, most, skew, False)
    places = jnp.arange(number_of)

    def named(sizes, turn):
        used = int((sizes > 0).sum())
        fixed = max(1, used // 4)
        shifted = fixed + (places - fixed + turn * (used - fixed)) % max(1, number_of - fixed)
        return jnp.zeros((number_of,), jnp.int32).at[sequence[jnp.where(places < fixed, places, shifted)]].set(jnp.asarray(sizes, jnp.int32))

    sizes = jnp.where(number % 4 == 0, named(packed, number // 4), named(ordinary, number - number // 4 - 1))
    mixed = jax.random.permutation(jax.random.fold_in(own, 3), number_of)
    source_of, sink = mixed[0:number_of // 2 * 2:2], mixed[1:number_of // 2 * 2:2]
    room = jnp.minimum(sizes[source_of] - 1, most - sizes[sink]) // 2
    room = jnp.where((source_of == sequence[0]) | (sink == sequence[0]) | (sizes[sink] == 0), 0, jnp.maximum(room, 0))
    shifted = jax.random.randint(jax.random.fold_in(own, 4), (number_of // 2,), 0, 1 << 20) % (room + 1)
    sizes = sizes.at[source_of].add(-shifted).at[sink].add(shifted)
    labels = jnp.searchsorted(jnp.cumsum(sizes), jnp.arange(rows * top), side="right").astype(jnp.int32)
    listing = labels.reshape(top, rows).T
    listing = listing[jax.random.permutation(jax.random.fold_in(own, 1), rows)]
    turn = jax.random.randint(jax.random.fold_in(own, 2), (rows, 1), 0, top)
    return jnp.take_along_axis(listing, (jnp.arange(top)[None, :] + turn) % top, axis=1)


def portions_of(count, total, most, skew, full):
    loads = [(1 << 20) // math.isqrt(grade ** skew) + 1 for grade in range(1, count + 1)]
    largest = most if full else min(most, max(-(-total // count), total * loads[0] // sum(loads)))
    least = 1 if total - largest >= count - 1 else 0
    holding, rest = [largest] + [least] * (count - 1), total - largest - least * (count - 1)
    while rest > 0:
        candidates = [i for i in range(1, count) if holding[i] < largest] or [i for i in range(1, count) if holding[i] < most]
        whole, remaining = sum([loads[i] for i in candidates]), rest
        for i in candidates:
            more = min(most - holding[i], max(1, remaining * loads[i] // whole), rest)
            holding[i] = holding[i] + more
            rest = rest - more
    return np.array(holding)


def normal_values(stream_key, extent, scale, bound, pieces=(), held_as=jnp.bfloat16):
    array = jax.random.normal(stream_key, extent, jnp.float32) * scale
    if len(pieces) > 0:
        array = level_of(stream_key, extent, pieces, -0.22, 0.18) * array
    return jnp.clip(array, min=-bound, max=bound).astype(held_as)


def setup_inputs(seed: int = 0) -> dict:
    key_of = jax.random.split(jax.random.key(seed), 6)
    grad_out = normal_values(key_of[0], (TOKENS, D), 1.0, 6.0, ((0, 256),))
    top_logits = draw_top_logits(jax.random.fold_in(key_of[5], 71), 0)
    expert_ids_keys = jax.random.split(jax.random.fold_in(key_of[2], 1), TOKENS // TOK_DEV)
    expert_ids_turns = jax.random.permutation(jax.random.fold_in(key_of[2], 3), TOKENS // TOK_DEV)
    expert_ids = jax.vmap(lambda own, number: shared_out(jax.random.fold_in(key_of[2], 2), own, number, TOK_DEV, EXPERTS, TOPK, CAP, 2))(expert_ids_keys, expert_ids_turns).reshape((TOKENS, TOPK))
    saved_hidden = normal_values(key_of[3], (N_CTX, EXPERTS, SLOTS, FF), 0.05, 0.29882812, ((0, 32), (1, 8)))
    w_down = normal_values(key_of[4], (EXPERTS, FF, D), FF ** -0.5, 0.15625, ((0, 8), (1, 32)))
    return dict(grad_out=grad_out, top_logits=top_logits, expert_ids=expert_ids, saved_hidden=saved_hidden, w_down=w_down)


def reference(grad_out, top_logits, expert_ids, saved_hidden, w_down):
    highest = lax.Precision.HIGHEST
    gate_probs = jax.nn.softmax(top_logits, axis=-1)
    gate_sent = lax.optimization_barrier(gate_probs.astype(jnp.bfloat16)).astype(jnp.float32)
    id_blocks = expert_ids.reshape(N_CTX, N_EXP, TOK_DEV, TOPK)
    row_blocks = grad_out.reshape(N_CTX, N_EXP, TOK_DEV, D)
    gate_blocks = gate_sent.reshape(N_CTX, N_EXP, TOK_DEV, TOPK)
    weights_wide = w_down.astype(jnp.float32)
    columns = jnp.arange(EXPERTS, dtype=jnp.int32)
    slot_iota = jnp.arange(CAP, dtype=jnp.int32)

    def one_group(carry, inputs):
        ids_group, rows_group, gate_group, hidden_group = inputs
        matches = ids_group[..., None] == columns
        onehot = matches.astype(jnp.float32)
        per_token = jnp.sum(matches.astype(jnp.int32), axis=2)
        rank_table = jnp.cumsum(per_token, axis=1) - per_token
        select = ((per_token[..., None] == 1) & (rank_table[..., None] == slot_iota)).astype(jnp.float32)
        gate_by_expert = jnp.sum(onehot * gate_group[..., None], axis=2)
        rows_in = jnp.einsum("stec,std->escd", select, rows_group.astype(jnp.float32), precision=highest).reshape(EXPERTS, SLOTS, D)
        gate_in = jnp.einsum("stec,ste->esc", select, gate_by_expert, precision=highest).reshape(EXPERTS, SLOTS, 1)
        backprop = jnp.einsum("esd,efd->esf", rows_in, weights_wide)
        hidden_wide = hidden_group.astype(jnp.float32)
        hidden_grad = (gate_in * backprop).astype(jnp.bfloat16)
        slot_grad = jnp.sum(hidden_wide * backprop, axis=2).reshape(EXPERTS, N_EXP, CAP)
        scaled = lax.optimization_barrier((gate_in * rows_in).astype(jnp.bfloat16)).astype(jnp.float32)
        carry = carry + jnp.einsum("esf,esd->efd", hidden_wide, scaled)
        by_expert = jnp.einsum("stec,esc->ste", select, slot_grad, precision=highest)
        gate_grad = jnp.sum(onehot * by_expert[:, :, None, :], axis=3)
        return carry, (hidden_grad, gate_grad)

    zero_grad = jnp.zeros((EXPERTS, FF, D), jnp.float32)
    down_grad, (hidden_grad, gate_grad) = lax.scan(one_group, zero_grad, (id_blocks, row_blocks, gate_blocks, saved_hidden))
    gate_grad = gate_grad.reshape(TOKENS, TOPK)
    logit_grad = gate_probs * (gate_grad - jnp.sum(gate_probs * gate_grad, axis=1, keepdims=True))
    return logit_grad, hidden_grad, down_grad
```

```python
import functools

import jax
import jax.numpy as jnp
from jax import lax
from jax.experimental import pallas as pl
from jax.experimental.pallas import tpu as pltpu
from jax.sharding import PartitionSpec as P

F32, BF16 = jnp.float32, jnp.bfloat16
LANES = 128
MESH = pl.DeviceIdType.MESH

RZ = (0, 1, -1, 2, -2, 3, -3, 4)
RX = (0, 1, -1, 2)


def out_edges(part, rz, rx):
    along_z, along_x = [], []
    if rz == 0:
        along_z = ["zF", "zR"]
    elif 0 < rz < 4:
        along_z = ["zF"]
    elif -3 < rz < 0:
        along_z = ["zR"]
    if rx == 0:
        along_x = ["xF", "xR"]
    elif rx == 1:
        along_x = ["xF"]
    if part == "A":
        return (along_x if rz == 0 else []) + along_z
    return (along_z if rx == 0 else []) + along_x


def parent_of(part, rz, rx):
    via_z = rz != 0 if part == "A" else rx == 0
    if via_z:
        return "zR" if rz > 0 else "zF"
    return "xR" if rx > 0 else "xF"


def moved(rz, rx, direction):
    step = 1 if direction[1] == "F" else -1
    return (rz + step, rx) if direction[0] == "z" else (rz, rx + step)


NODES = [(rz, rx) for rz in RZ for rx in RX]
SUM_SLOT = {}
SEND_ID = {}
for _part in "AB":
    _n = 0
    for _rz, _rx in NODES:
        for _d in out_edges(_part, _rz, _rx):
            SUM_SLOT[_part, _rz, _rx, _d] = _n
            SEND_ID[_part, _rz, _rx, _d] = _n
            _n += 1
N_EDGES = 31


def plan(bytes_a, bytes_b, bytes_half, costs, rate=85.0, hop=1.7, sibling_rate=300.0):
    size = {"A": bytes_a / 1e3, "B": bytes_b / 1e3, "y": bytes_half / 1e3}
    queues = {d: [] for d in ("zF", "zR", "xF", "xR", "yF", "yR", "ss")}
    arrivals, clock, order = [], [0.0], []
    have = set()

    def send(direction, kind, tag):
        queues[direction].append([size[kind], tag])

    def rate_of(direction):
        if direction == "ss":
            return sibling_rate
        other = direction[0] + ("R" if direction[1] == "F" else "F")
        return rate / 2 if queues[other] else rate

    def advance(until):
        while clock[0] < until - 1e-9:
            step = until - clock[0]
            for d, q in queues.items():
                if q:
                    step = min(step, q[0][0] / rate_of(d))
            rates = {d: rate_of(d) for d in queues}
            for d, q in queues.items():
                if q:
                    q[0][0] -= step * rates[d]
            clock[0] += step
            for d, q in queues.items():
                if q and q[0][0] <= 1e-6:
                    arrivals.append((clock[0] + hop, q.pop(0)[1]))

    pending = []

    def task(priority, name, needs, action=None, cost=0.1, pace=None, compute=False):
        pending.append([priority, name, frozenset(needs), action or (lambda: None), cost, pace, compute])

    def start():
        for d in ("xF", "xR"):
            send(d, "A", ("agA", *moved(0, 0, d)))
        for d in ("zF", "zR"):
            send(d, "B", ("agB", *moved(0, 0, d)))
        for d in ("xF", "xR"):
            send(d, "B", ("agB", *moved(0, 0, d)))
        for d in ("zF", "zR"):
            send(d, "A", ("agA", *moved(0, 0, d)))
        for h in (0, 1):
            send("yF", "y", ("y", 1, h))
            send("yR", "y", ("y", -1, h))
            send("ss", "y", ("s", 0, h))

    task(0, ("start",), [], start, costs["start"])

    def gather_event(part, rz, rx):
        def act():
            for d in out_edges(part, rz, rx):
                send(d, part, ("ag" + part, *moved(rz, rx, d)))
        task(1, ("ag", part, rz, rx), [("ag" + part, rz, rx)], act, 0.1)

    for part in "AB":
        for rz, rx in NODES:
            if (rz, rx) != (0, 0):
                gather_event(part, rz, rx)

    def y_event(ry, h):
        def act():
            if ry == 1:
                send("yF", "y", ("y", 2, h))
            send("ss", "y", ("s", ry, h))
        task(1, ("y", ry, h), [("y", ry, h)], act, 0.1)

    for ry in (1, -1, 2):
        for h in (0, 1):
            y_event(ry, h)
    for ry in (0, 1, -1, 2):
        for h in (0, 1):
            task(1, ("s", ry, h), [("s", ry, h)])
    task(3, ("meta",), [("done", "start")], cost=costs["meta"], compute=True)
    for i in range(costs["n_turn"]):
        task(5, ("turn", i), [("done", "meta")], cost=costs["turn"], compute=True)
    for own in (1, 0):
        for ry in (0, 1, -1, 2):
            needs = [("done", "meta")]
            if own and ry:
                needs += [("done", "y", ry, 0), ("done", "y", ry, 1)]
            if not own:
                needs += [("done", "s", ry, 0), ("done", "s", ry, 1)]
            task(4, ("sel", own, ry), needs, cost=costs["sel"], compute=True)
    sels = [("done", "sel", own, ry) for own in (1, 0) for ry in (0, 1, -1, 2)]
    turns = [("done", "turn", i) for i in range(costs["n_turn"])]
    for i, cost in enumerate(costs["pa"]):
        task(6 + 0.01 * i, ("pa", i), sels + turns, cost=cost, compute=True)
    pas = [("done", "pa", i) for i in range(len(costs["pa"]))]
    for i, cost in enumerate(costs["pb"]):
        task(7 + 0.01 * i, ("pb", i), sels + turns + pas, cost=cost, compute=True)
    pbs = [("done", "pb", i) for i in range(len(costs["pb"]))]

    def sum_event(part, rz, rx):
        kids = out_edges(part, rz, rx)
        needs = (pas if part == "A" else pbs) + [("rs" + part, rz, rx, d) for d in kids]
        towards = None if (rz, rx) == (0, 0) else parent_of(part, rz, rx)

        def act():
            if towards is not None:
                back = towards[0] + ("R" if towards[1] == "F" else "F")
                up = {"z": (rz - 1 if back[1] == "F" else rz + 1, rx), "x": (rz, rx - 1 if back[1] == "F" else rx + 1)}[back[0]]
                send(towards, part, ("rs" + part, *up, back))
        far = abs(rz) * 2 + abs(rx)
        task(1 if kids else 2 - 0.01 * far, ("rs", part, rz, rx), needs, act, 0.3 if kids else 0.05, None if kids else towards)

    for part in "AB":
        for rz, rx in NODES:
            sum_event(part, rz, rx)
    gathered = [("done", "ag", part, rz, rx) for part in "AB" for rz, rx in NODES if (rz, rx) != (0, 0)]
    for i in range(costs["n_back"]):
        task(8 + 0.01 * i, ("back", i), sels + gathered, cost=costs["back"], compute=True)
    task(2.5, ("give",), [("done", "back", i) for i in range(costs["n_back"])], cost=1.0, compute=True)
    task(9, ("logit",), [("done", "give")] + [("done", "rs", "B", rz, rx) for rz, rx in NODES[1:]], cost=1.0, compute=True)

    trace = []
    while pending:
        for a in [a for a in arrivals if a[0] <= clock[0] + 1e-9]:
            arrivals.remove(a)
            have.add(a[1])
        ready = [t for t in pending if t[2] <= have and (t[5] is None or len(queues[t[5]]) < 2)]
        if not ready:
            times = [a[0] for a in arrivals]
            nxt = min(times) if times else clock[0] + 0.5
            advance(min(nxt, clock[0] + 0.25))
            continue
        best = min(ready, key=lambda t: t[0])
        pending.remove(best)
        trace.append((round(clock[0], 2), best[1]))
        best[3]()
        advance(clock[0] + best[4])
        have.add(("done", *best[1]))
    return [name for _, name in trace], trace


def body(sizes, order, *refs):
    (n_z, n_x, n_y, tokens, width, padded, cut, shard, cap, top, experts, mm, pa_cols, pb_cols) = sizes
    (go_ref, lg_ref, ids_ref, hid_ref, w_ref, lo_ref, hg_ref, dg_ref,
     w_all, p_all, tok, rows, scl, hid_t, sum_a, sum_b, meta, ret_in, ret_out, gate, sgrad,
     ag_s, ag_r, rs_s, rs_r, y_s, y_r, sib_s, sib_r, meta_s, meta_r, ret_s, ret_r) = refs
    ctx, exp = lax.axis_index("ctx"), lax.axis_index("exp")
    z, x, y, core = ctx // n_x, ctx % n_x, exp // 2, exp % 2
    sense = 1 - 2 * core
    half = tokens // 2

    def ctx_dev(zz, xx):
        return (lax.rem(zz + 2 * n_z, n_z) * n_x + lax.rem(xx + 2 * n_x, n_x), exp)

    def exp_dev(yy, cc):
        return (ctx, lax.rem(yy + 2 * n_y, n_y) * 2 + cc)

    peer = {
        "zF": ctx_dev(z + sense, x), "zR": ctx_dev(z - sense, x),
        "xF": ctx_dev(z, x + sense), "xR": ctx_dev(z, x - sense),
        "yF": exp_dev(y + sense, core), "yR": exp_dev(y - sense, core),
        "ss": exp_dev(y, 1 - core),
    }
    others = [(ctx, lax.rem(exp + k, experts)) for k in range(1, experts)]
    barrier = pltpu.get_barrier_semaphore()
    greeted = [peer["zF"], peer["zR"], peer["xF"], peer["xR"]] + others
    for dev in greeted:
        pl.semaphore_signal(barrier, inc=1, device_id=dev, device_id_type=MESH)

    def shard_rows(rz, rx):
        zz = lax.rem(z - sense * rz + 2 * n_z, n_z)
        xx = lax.rem(x - sense * rx + 2 * n_x, n_x)
        return pl.ds(pl.multiple_of((zz * n_x + xx) * shard, shard), shard)

    cols = {"A": pl.ds(0, cut), "B": pl.ds(cut, padded - cut)}
    sums = {"A": sum_a, "B": sum_b}
    which = {"A": 0, "B": 1}
    sends = []

    def remote(src, dst, s_sem, r_sem, dev):
        return pltpu.make_async_remote_copy(
            src_ref=src, dst_ref=dst, send_sem=s_sem, recv_sem=r_sem, device_id=dev, device_id_type=MESH
        )

    def push(*args):
        copy = remote(*args)
        copy.start()
        sends.append(copy)

    def gather_recv_sem(part, rz, rx):
        return ag_r.at[which[part], NODES.index((rz, rx))]

    def gather_pass(part, rz, rx, directions):
        ref = w_all.at[shard_rows(rz, rx), cols[part]]
        for d in directions:
            push(ref, ref, ag_s.at[which[part], SEND_ID[part, rz, rx, d]], gather_recv_sem(part, *moved(rz, rx, d)), peer[d])

    def gather_event(part, rz, rx):
        ref = w_all.at[shard_rows(rz, rx), cols[part]]
        remote(ref, ref, ag_s.at[0, 0], gather_recv_sem(part, rz, rx), peer["zF"]).wait_recv()
        gather_pass(part, rz, rx, out_edges(part, rz, rx))

    Y_INDEX = {0: 0, 1: 1, -1: 2, 2: 3}

    def block_of(own, ry):
        yy = lax.rem(y - sense * ry + 2 * n_y, n_y) if own else lax.rem(y + sense * ry + 2 * n_y, n_y)
        return yy * 2 + (core if own else 1 - core)

    def half_ref(own, ry, h):
        return tok.at[block_of(own, ry), pl.ds(h * half, half)]

    def y_push(ry, h, d):
        ref = half_ref(True, ry, h)
        to = ry + (1 if d == "yF" else -1)
        push(ref, ref, y_s.at[{"yF": ry, "yR": 2}[d], h], y_r.at[Y_INDEX[to], h], peer[d])

    def sib_push(ry, h):
        ref = half_ref(True, ry, h)
        push(ref, ref, sib_s.at[Y_INDEX[ry], h], sib_r.at[Y_INDEX[ry], h], peer["ss"])

    def y_event(ry, h):
        ref = half_ref(True, ry, h)
        remote(ref, ref, y_s.at[0, 0], y_r.at[Y_INDEX[ry], h], peer["yF"]).wait_recv()
        if ry == 1:
            y_push(1, h, "yF")
        sib_push(ry, h)

    def s_event(ry, h):
        ref = half_ref(False, ry, h)
        remote(ref, ref, y_s.at[0, 0], sib_r.at[Y_INDEX[ry], h], peer["ss"]).wait_recv()

    def start():
        tail = width // LANES * LANES
        me = block_of(True, 0)
        tok[me, :, pl.ds(tail, padded - tail)] = jnp.zeros((tokens, padded - tail), BF16)
        tok[me, :, pl.ds(0, width)] = go_ref[...]
        mine = shard_rows(0, 0)
        w_all[mine, pl.ds(tail, padded - tail)] = jnp.zeros((shard, padded - tail), BF16)
        w_all[mine, pl.ds(0, width)] = w_ref[...]
        pl.semaphore_wait(barrier, len(greeted))
        gather_pass("A", 0, 0, ["xF", "xR"])
        gather_pass("B", 0, 0, ["zF", "zR"])
        gather_pass("B", 0, 0, ["xF", "xR"])
        gather_pass("A", 0, 0, ["zF", "zR"])
        for h in (0, 1):
            y_push(0, h, "yF")
            y_push(0, h, "yR")
            sib_push(0, h)

    def gate_probs():
        logits = lg_ref[...]
        weights = jnp.exp(logits - jnp.max(logits, axis=1, keepdims=True))
        return weights / jnp.sum(weights, axis=1, keepdims=True)

    def matches():
        lane = lax.broadcasted_iota(jnp.int32, (tokens, LANES), 1)
        ids = ids_ref[...]
        return [ids[:, k:k + 1] == lane for k in range(top)]

    def meta_task():
        sent = gate_probs().astype(BF16).astype(F32)
        chosen = jnp.zeros((tokens, LANES), F32)
        by_expert = jnp.zeros((tokens, LANES), F32)
        for k, match in enumerate(matches()):
            chosen = chosen + jnp.where(match, 1.0, 0.0)
            by_expert = by_expert + jnp.where(match, sent[:, k:k + 1], 0.0)
        earlier = lax.broadcasted_iota(jnp.int32, (tokens, tokens), 0) > lax.broadcasted_iota(jnp.int32, (tokens, tokens), 1)
        rank = jnp.dot(jnp.where(earlier, 1.0, 0.0).astype(BF16), chosen.astype(BF16), preferred_element_type=F32)
        rank = jnp.where(chosen > 0.5, rank, -1.0)
        meta[exp, pl.ds(0, experts), :] = rank.T[0:experts, :]
        meta[exp, pl.ds(experts, experts), :] = by_expert.T[0:experts, :]

    def meta_send():
        for k in range(1, experts):
            push(meta.at[exp], meta.at[exp], meta_s.at[k - 1], meta_r.at[k - 1], others[k - 1])

    def meta_wait():
        for k in range(1, experts):
            src = lax.rem(exp - k + experts, experts)
            remote(meta.at[src], meta.at[src], meta_s.at[0], meta_r.at[k - 1], others[0]).wait_recv()

    def select_of(s):
        rank = meta[s, pl.ds(exp, 1), :]
        slot = lax.broadcasted_iota(jnp.int32, (cap, tokens), 0).astype(F32)
        return rank == slot

    def sel_task(own, ry):
        s = block_of(own, ry)
        select = select_of(s)
        gates = jnp.sum(jnp.where(select, meta[s, pl.ds(experts + exp, 1), :], 0.0), axis=1, keepdims=True)
        at = pl.ds(pl.multiple_of(s * cap, cap), cap)
        gate[at, :] = jnp.broadcast_to(gates, (cap, LANES))
        picked = jnp.dot(jnp.where(select, 1.0, 0.0).astype(BF16), tok[s], preferred_element_type=F32)
        rows[at, :] = picked.astype(BF16)
        scl[at, :] = (gates * picked).astype(BF16)

    slots = experts * cap
    n_f = hid_ref.shape[1]

    def turn_task(i):
        span = n_f // mm["n_turn"]
        hid_t[pl.ds(i * span, span), :] = hid_ref[:, pl.ds(i * span, span)].T

    def grad_cols(at, span):
        p_all[:, pl.ds(at, span)] = jnp.dot(hid_t[...], scl[:, pl.ds(at, span)], preferred_element_type=F32).astype(BF16)

    def grad_task(base, count, span):
        if count == 1:
            grad_cols(base, span)
            return

        def step(i, _):
            grad_cols(pl.multiple_of(base + i * span, LANES), span)
            return 0
        lax.fori_loop(0, count, step, 0)

    def sum_event(part, rz, rx):
        kids = out_edges(part, rz, rx)
        mine = p_all.at[shard_rows(rz, rx), cols[part]]
        src = mine
        if kids:
            total = mine[...].astype(F32)
            for d in kids:
                slot = SUM_SLOT[part, rz, rx, d]
                ref = sums[part].at[slot]
                remote(ref, ref, rs_s.at[0, 0], rs_r.at[which[part], slot], peer["zF"]).wait_recv()
                total = total + ref[...].astype(F32)
            if (rz, rx) == (0, 0):
                if part == "A":
                    dg_ref[:, pl.ds(0, cut)] = total
                else:
                    dg_ref[:, pl.ds(cut, width - cut)] = total[:, 0:width - cut]
                return
            src = sums[part].at[SUM_SLOT[part, rz, rx, kids[0]]]
            src[...] = total.astype(BF16)
        towards = parent_of(part, rz, rx)
        back = towards[0] + ("R" if towards[1] == "F" else "F")
        step = -1 if back[1] == "F" else 1
        up = (rz + step, rx) if back[0] == "z" else (rz, rx + step)
        slot = SUM_SLOT[part, *up, back]
        push(src, sums[part].at[slot], rs_s.at[which[part], slot], rs_r.at[which[part], slot], peer[towards])

    def back_cols(at, span, first):
        prod = lax.dot_general(rows[...], w_all[pl.ds(at, span), :], (((1,), (1,)), ((), ())), preferred_element_type=F32)
        hg_ref[:, pl.ds(at, span)] = (gate[:, 0:1] * prod).astype(BF16)
        weighted = hid_ref[:, pl.ds(at, span)].astype(F32) * prod
        part = weighted[:, 0:LANES]
        for j in range(1, span // LANES):
            part = part + weighted[:, j * LANES:(j + 1) * LANES]
        sgrad[...] = part if first else sgrad[...] + part

    def back_task(i):
        span = n_f // mm["n_back"]
        back_cols(i * span, span, i == 0)

    def give_task():
        for k in range(experts):
            s = lax.rem(exp + k, experts)
            total = jnp.sum(sgrad[pl.ds(pl.multiple_of(s * cap, cap), cap), :], axis=1, keepdims=True)
            row = jnp.sum(jnp.where(select_of(s), total, 0.0), axis=0, keepdims=True)
            if k == 0:
                ret_in[exp] = jnp.broadcast_to(row, (8, tokens))
            else:
                ret_out[k - 1] = jnp.broadcast_to(row, (8, tokens))
        for k in range(1, experts):
            push(ret_out.at[k - 1], ret_in.at[exp], ret_s.at[k - 1], ret_r.at[k - 1], others[k - 1])

    def logit_task():
        for k in range(1, experts):
            src = lax.rem(exp - k + experts, experts)
            remote(ret_in.at[src], ret_in.at[src], ret_s.at[0], ret_r.at[k - 1], others[0]).wait_recv()
        by_expert = jnp.concatenate(
            [ret_in[e, 0:1, :] for e in range(experts)] + [jnp.zeros((tokens - experts, tokens), F32)], axis=0
        ).T
        probs = gate_probs()
        grads = [jnp.sum(jnp.where(m, by_expert, 0.0), axis=1, keepdims=True) for m in matches()]
        mean = sum(probs[:, k:k + 1] * g for k, g in enumerate(grads))
        for k, g in enumerate(grads):
            lo_ref[:, k:k + 1] = probs[:, k:k + 1] * (g - mean)

    sent_meta = [False, False]
    for name in order:
        kind = name[0]
        if kind == "start":
            start()
        elif kind == "meta":
            meta_task()
        elif kind == "ag":
            gather_event(*name[1:])
        elif kind == "y":
            y_event(*name[1:])
        elif kind == "s":
            s_event(*name[1:])
        elif kind == "turn":
            turn_task(name[1])
            if not sent_meta[0]:
                meta_send()
                sent_meta[0] = True
        elif kind == "sel":
            if not sent_meta[0]:
                meta_send()
                sent_meta[0] = True
            if not sent_meta[1] and name[1:] != (1, 0):
                meta_wait()
                sent_meta[1] = True
            sel_task(*name[1:])
        elif kind == "pa":
            grad_task(*pa_cols[name[1]])
        elif kind == "pb":
            grad_task(*pb_cols[name[1]])
        elif kind == "rs":
            sum_event(*name[1:])
        elif kind == "back":
            back_task(name[1])
        elif kind == "give":
            give_task()
        elif kind == "logit":
            logit_task()
    for copy in sends:
        copy.wait_send()


def per_device(grad_out, top_logits, expert_ids, saved_hidden, w_down):
    n_z, n_x, n_y = 8, 4, 4
    tokens, width = grad_out.shape
    slots, n_f = saved_hidden.shape[2:]
    shard = w_down.shape[1]
    top = top_logits.shape[1]
    experts = n_y * 2
    cap = slots // experts
    padded = -(-width // LANES) * LANES
    cut = padded * 9 // 23 // LANES * LANES
    span = 256

    def pieces(base, end, groups):
        whole = (end - base) // span
        out = []
        at = base
        for g in range(groups):
            count = whole * (g + 1) // groups - whole * g // groups
            if count:
                out.append((at, count, span))
                at += count * span
        if at < end:
            out.append((at, 1, end - at))
        return out

    pa_cols, pb_cols = pieces(0, cut, 2), pieces(cut, padded, 3)
    mm = {"n_turn": 6, "n_back": 6}
    chunk = 1.0
    costs = {
        "start": 0.5, "meta": 1.5, "turn": 0.6, "n_turn": mm["n_turn"], "sel": 0.9,
        "pa": [chunk * c for _, c, _ in pa_cols], "pb": [chunk * c for _, c, _ in pb_cols],
        "back": 2.0, "n_back": mm["n_back"],
    }
    order, _ = plan(shard * cut * 2, shard * (padded - cut) * 2, tokens // 2 * padded * 2, costs)
    sizes = (n_z, n_x, n_y, tokens, width, padded, cut, shard, cap, top, experts, mm, pa_cols, pb_cols)
    vmem = pl.BlockSpec(memory_space=pltpu.VMEM)
    dma = pltpu.SemaphoreType.DMA
    logit, hidden_grad, down_grad = pl.pallas_call(
        functools.partial(body, sizes, order),
        out_shape=(
            jax.ShapeDtypeStruct((tokens, top), F32),
            jax.ShapeDtypeStruct((slots, n_f), BF16),
            jax.ShapeDtypeStruct((shard, width), F32),
        ),
        in_specs=[vmem] * 5,
        out_specs=(vmem, vmem, vmem),
        scratch_shapes=[
            pltpu.VMEM((n_f, padded), BF16),
            pltpu.VMEM((n_f, padded), BF16),
            pltpu.VMEM((experts, tokens, padded), BF16),
            pltpu.VMEM((slots, padded), BF16),
            pltpu.VMEM((slots, padded), BF16),
            pltpu.VMEM((n_f, slots), BF16),
            pltpu.VMEM((N_EDGES, shard, cut), BF16),
            pltpu.VMEM((N_EDGES, shard, padded - cut), BF16),
            pltpu.VMEM((experts, 2 * experts, tokens), F32),
            pltpu.VMEM((experts, 8, tokens), F32),
            pltpu.VMEM((experts, 8, tokens), F32),
            pltpu.VMEM((slots, LANES), F32),
            pltpu.VMEM((slots, LANES), F32),
            dma((2, N_EDGES)), dma((2, len(NODES))),
            dma((2, N_EDGES)), dma((2, N_EDGES)),
            dma((3, 2)), dma((4, 2)), dma((4, 2)), dma((4, 2)),
            dma((experts - 1,)), dma((experts - 1,)), dma((experts - 1,)), dma((experts - 1,)),
        ],
        compiler_params=pltpu.CompilerParams(collective_id=0, has_side_effects=True, vmem_limit_bytes=63000 * 1024),
    )(grad_out, top_logits, expert_ids, saved_hidden[0, 0], w_down[0])
    return (logit, hidden_grad[None, None], down_grad[None])


def solution(mesh):
    return jax.shard_map(
        per_device,
        mesh=mesh,
        in_specs=(
            P(("ctx", "exp"), None),
            P(("ctx", "exp"), None),
            P(("ctx", "exp"), None),
            P("ctx", "exp", None, None),
            P("exp", "ctx", None),
        ),
        out_specs=(P(("ctx", "exp"), None), P("ctx", "exp", None, None), P("exp", "ctx", None)),
        check_vma=False,
    )
```

```python
import functools

import jax
import jax.numpy as jnp
from jax import lax
from jax.experimental import pallas as pl
from jax.experimental.pallas import tpu as pltpu
from jax.sharding import PartitionSpec as P

F32, BF16 = jnp.float32, jnp.bfloat16
LANES = 128
MESH = pl.DeviceIdType.MESH

RZ = (0, 1, -1, 2, -2, 3, -3, 4)
RX = (0, 1, -1, 2)


def out_edges(part, rz, rx):
    along_z, along_x = [], []
    if rz == 0:
        along_z = ["zF", "zR"]
    elif 0 < rz < 4:
        along_z = ["zF"]
    elif -3 < rz < 0:
        along_z = ["zR"]
    if rx == 0:
        along_x = ["xF", "xR"]
    elif rx == 1:
        along_x = ["xF"]
    if part == "A":
        return (along_x if rz == 0 else []) + along_z
    return (along_z if rx == 0 else []) + along_x


def parent_of(part, rz, rx):
    via_z = rz != 0 if part == "A" else rx == 0
    if via_z:
        return "zR" if rz > 0 else "zF"
    return "xR" if rx > 0 else "xF"


def moved(rz, rx, direction):
    step = 1 if direction[1] == "F" else -1
    return (rz + step, rx) if direction[0] == "z" else (rz, rx + step)


NODES = [(rz, rx) for rz in RZ for rx in RX]
SUM_SLOT = {}
SEND_ID = {}
for _part in "AB":
    _n = 0
    for _rz, _rx in NODES:
        for _d in out_edges(_part, _rz, _rx):
            SUM_SLOT[_part, _rz, _rx, _d] = _n
            SEND_ID[_part, _rz, _rx, _d] = _n
            _n += 1
N_EDGES = 31


def sum_target(part, rz, rx):
    towards = parent_of(part, rz, rx)
    back = towards[0] + ("R" if towards[1] == "F" else "F")
    step = -1 if back[1] == "F" else 1
    up = (rz + step, rx) if back[0] == "z" else (rz, rx + step)
    return towards, SUM_SLOT[part, *up, back]


def task_list(n_turn, n_pa, n_pb, n_back):
    out = [("start",), ("meta",), ("msend",), ("mwait",), ("give",), ("logit",)]
    for part in "AB":
        for rz, rx in NODES:
            if (rz, rx) != (0, 0):
                out.append(("aw", part, rz, rx))
            out += [("ap", part, rz, rx, d) for d in out_edges(part, rz, rx)]
    for part in "AB":
        for rz, rx in NODES:
            if out_edges(part, rz, rx):
                out.append(("rs", part, rz, rx))
            if (rz, rx) != (0, 0):
                out.append(("rp", part, rz, rx))
    for h in (0, 1):
        out += [("yp", 0, h, "yF"), ("yp", 0, h, "yR"), ("yp", 0, h, "ss")]
        for ry in (1, -1, 2):
            out.append(("yw", ry, h))
            out.append(("yp", ry, h, "ss"))
        out.append(("yp", 1, h, "yF"))
        out += [("sw", ry, h) for ry in (0, 1, -1, 2)]
    for own in (1, 0):
        out += [("sel", own, ry) for ry in (0, 1, -1, 2)]
    out += [("turn", i) for i in range(n_turn)]
    out += [("pa", i) for i in range(n_pa)]
    out += [("pb", i) for i in range(n_pb)]
    out += [("back", i) for i in range(n_back)]
    return out


ORDER = [
    0, 70, 69, 233, 71, 232, 234, 7, 1, 2, 248, 6, 68, 9, 247, 8, 260, 242, 268, 269, 270, 271, 256, 272,
    84, 87, 85, 86, 273, 246, 72, 73, 74, 3, 264, 28, 29, 76, 78, 77, 79, 10, 12, 13, 14, 16, 15, 11,
    20, 237, 238, 100, 103, 235, 236, 241, 101, 21, 88, 90, 244, 44, 45, 89, 243, 92, 93, 95, 30, 31, 75, 82,
    22, 23, 94, 32, 251, 252, 249, 255, 262, 33, 24, 25, 80, 81, 261, 106, 250, 258, 266, 36, 116, 118, 17, 19,
    239, 18, 240, 117, 257, 265, 98, 60, 245, 37, 108, 111, 91, 46, 47, 110, 253, 254, 263, 109, 38, 121, 48, 49,
    259, 267, 96, 97, 274, 39, 40, 275, 34, 35, 114, 102, 276, 83, 26, 27, 277, 61, 278, 119, 120, 182, 184, 279,
    52, 280, 53, 62, 112, 113, 183, 281, 282, 99, 50, 123, 125, 124, 181, 177, 283, 104, 105, 284, 171, 54, 55, 51,
    285, 207, 225, 122, 219, 172, 212, 175, 42, 43, 128, 176, 173, 115, 64, 178, 231, 230, 174, 169, 161, 162, 204, 126,
    213, 170, 63, 41, 127, 65, 222, 155, 58, 59, 107, 156, 223, 218, 159, 163, 164, 160, 216, 217, 157, 145, 158, 206,
    146, 228, 56, 57, 153, 154, 229, 188, 139, 67, 140, 179, 210, 129, 143, 147, 211, 144, 148, 224, 141, 142, 180, 201,
    194, 137, 66, 138, 286, 287, 165, 200, 195, 288, 289, 226, 205, 227, 290, 167, 168, 291, 220, 221, 189, 4, 214, 215,
    166, 151, 152, 198, 199, 208, 209, 192, 193, 5, 149, 150, 202, 135, 203, 136, 186, 187, 133, 196, 197, 134, 190, 191,
    131, 132, 185, 130,
]


def body(sizes, order, *refs):
    (n_z, n_x, n_y, tokens, width, padded, cut, shard, cap, top, experts, spans) = sizes
    turns, pa_cols, pb_cols, backs = spans
    (go_hbm, lg_ref, ids_ref, hid_hbm, w_hbm, lo_ref, hg_hbm, dg_hbm,
     w_all, p_all, tok, rows, scl, hid, hid_t, hg, sum_a, sum_b, meta, ret_in, ret_out, gate, sgrad, go_ref, dg_ref,
     ag_s, ag_r, rs_s, rs_r, y_s, y_r, sib_s, sib_r, meta_s, meta_r, ret_s, ret_r, in_sem, hg_sem, dg_sem) = refs
    ctx, exp = lax.axis_index("ctx"), lax.axis_index("exp")
    z, x, y, core = ctx // n_x, ctx % n_x, exp // 2, exp % 2
    sense = 1 - 2 * core
    half = width // 2

    def ctx_dev(zz, xx):
        return (lax.rem(zz + 2 * n_z, n_z) * n_x + lax.rem(xx + 2 * n_x, n_x), exp)

    def exp_dev(yy, cc):
        return (ctx, lax.rem(yy + 2 * n_y, n_y) * 2 + cc)

    peer = {
        "zF": ctx_dev(z + sense, x), "zR": ctx_dev(z - sense, x),
        "xF": ctx_dev(z, x + sense), "xR": ctx_dev(z, x - sense),
        "yF": exp_dev(y + sense, core), "yR": exp_dev(y - sense, core),
        "ss": exp_dev(y, 1 - core),
    }
    others = [(ctx, lax.rem(exp + k, experts)) for k in range(1, experts)]
    slots = experts * cap
    barrier = pltpu.get_barrier_semaphore()
    greeted = [peer["zF"], peer["zR"], peer["xF"], peer["xR"]] + others
    for dev in greeted:
        pl.semaphore_signal(barrier, inc=1, device_id=dev, device_id_type=MESH)

    def shard_rows(rz, rx):
        zz = lax.rem(z - sense * rz + 2 * n_z, n_z)
        xx = lax.rem(x - sense * rx + 2 * n_x, n_x)
        return pl.ds(pl.multiple_of((zz * n_x + xx) * shard, shard), shard)

    cols = {"A": pl.ds(0, cut), "B": pl.ds(cut, padded - cut)}
    sums = {"A": sum_a, "B": sum_b}
    which = {"A": 0, "B": 1}
    sends = []

    def remote(src, dst, s_sem, r_sem, dev):
        return pltpu.make_async_remote_copy(
            src_ref=src, dst_ref=dst, send_sem=s_sem, recv_sem=r_sem, device_id=dev, device_id_type=MESH
        )

    def push(*args):
        copy = remote(*args)
        copy.start()
        sends.append(copy)

    def gather_recv_sem(part, rz, rx):
        return ag_r.at[which[part], NODES.index((rz, rx))]

    def gather_pass(part, rz, rx, d):
        ref = w_all.at[shard_rows(rz, rx), cols[part]]
        push(ref, ref, ag_s.at[which[part], SEND_ID[part, rz, rx, d]], gather_recv_sem(part, *moved(rz, rx, d)), peer[d])

    def gather_wait(part, rz, rx):
        ref = w_all.at[shard_rows(rz, rx), cols[part]]
        remote(ref, ref, ag_s.at[0, 0], gather_recv_sem(part, rz, rx), peer["zF"]).wait_recv()

    Y_INDEX = {0: 0, 1: 1, -1: 2, 2: 3}

    def block_of(own, ry):
        yy = lax.rem(y - sense * ry + 2 * n_y, n_y) if own else lax.rem(y + sense * ry + 2 * n_y, n_y)
        return yy * 2 + (core if own else 1 - core)

    def half_ref(own, ry, h):
        return tok.at[block_of(own, ry), pl.ds(h * half, half)]

    def y_push(ry, h, d):
        ref = half_ref(True, ry, h)
        src = go_ref.at[pl.ds(h * half, half)] if ry == 0 else ref
        if d == "ss":
            push(src, ref, sib_s.at[Y_INDEX[ry], h], sib_r.at[Y_INDEX[ry], h], peer["ss"])
            return
        to = ry + (1 if d == "yF" else -1)
        push(src, ref, y_s.at[{"yF": ry, "yR": 2}[d], h], y_r.at[Y_INDEX[to], h], peer[d])

    def y_wait(ry, h):
        ref = half_ref(True, ry, h)
        remote(ref, ref, y_s.at[0, 0], y_r.at[Y_INDEX[ry], h], peer["yF"]).wait_recv()

    def s_wait(ry, h):
        ref = half_ref(False, ry, h)
        remote(ref, ref, y_s.at[0, 0], sib_r.at[Y_INDEX[ry], h], peer["ss"]).wait_recv()

    loads = {
        "w": pltpu.make_async_copy(w_hbm, w_all.at[shard_rows(0, 0)], in_sem.at[0]),
        "go": pltpu.make_async_copy(go_hbm, go_ref, in_sem.at[1]),
        "hid": pltpu.make_async_copy(hid_hbm, hid, in_sem.at[2]),
    }

    def start():
        for name in ("w", "go", "hid"):
            loads[name].start()
        loads["w"].wait()
        loads["go"].wait()
        pl.semaphore_wait(barrier, len(greeted))

    def store_down_grad(i):
        at = (pl.ds(0, cut), pl.ds(cut, width - cut))[i]
        return pltpu.make_async_copy(dg_ref.at[:, at], dg_hbm.at[:, at], dg_sem.at[i])

    def gate_probs():
        logits = lg_ref[...]
        weights = jnp.exp(logits - jnp.max(logits, axis=0, keepdims=True))
        return weights / jnp.sum(weights, axis=0, keepdims=True)

    def matches():
        row = lax.broadcasted_iota(jnp.int32, (experts, tokens), 0)
        ids = ids_ref[...]
        return [ids[k:k + 1, :] == row for k in range(top)]

    def meta_task():
        sent = gate_probs().astype(BF16).astype(F32)
        chosen = jnp.zeros((experts, tokens), F32)
        by_expert = jnp.zeros((experts, tokens), F32)
        for k, match in enumerate(matches()):
            chosen = chosen + jnp.where(match, 1.0, 0.0)
            by_expert = by_expert + jnp.where(match, sent[k:k + 1, :], 0.0)
        earlier = lax.broadcasted_iota(jnp.int32, (tokens, tokens), 0) < lax.broadcasted_iota(jnp.int32, (tokens, tokens), 1)
        rank = jnp.dot(chosen.astype(BF16), jnp.where(earlier, 1.0, 0.0).astype(BF16), preferred_element_type=F32)
        meta[exp, pl.ds(0, experts), :] = jnp.where(chosen > 0.5, rank, -1.0)
        meta[exp, pl.ds(experts, experts), :] = by_expert

    def meta_send():
        for k in range(1, experts):
            push(meta.at[exp], meta.at[exp], meta_s.at[k - 1], meta_r.at[k - 1], others[k - 1])

    def meta_wait():
        for k in range(1, experts):
            src = lax.rem(exp - k + experts, experts)
            remote(meta.at[src], meta.at[src], meta_s.at[0], meta_r.at[k - 1], others[0]).wait_recv()

    def select_of(s):
        rank = meta[s, pl.ds(exp, 1), :]
        slot = lax.broadcasted_iota(jnp.int32, (cap, tokens), 0).astype(F32)
        return rank == slot

    def sel_task(own, ry):
        s = block_of(own, ry)
        select = select_of(s)
        gates = jnp.sum(jnp.where(select, meta[s, pl.ds(experts + exp, 1), :], 0.0), axis=1, keepdims=True)
        at = pl.ds(pl.multiple_of(s * cap, cap), cap)
        gate[at, :] = jnp.broadcast_to(gates, (cap, LANES))
        block = go_ref[...] if own and ry == 0 else tok[s]
        picked = lax.dot_general(
            jnp.where(select, 1.0, 0.0).astype(BF16), block, (((1,), (1,)), ((), ())), preferred_element_type=F32
        )
        rows[at, pl.ds(0, width)] = picked.astype(BF16)
        scl[at, pl.ds(0, width)] = (gates * picked).astype(BF16)

    def turn_task(at, span):
        hid_t[pl.ds(at, span), :] = hid[:, pl.ds(at, span)].T

    def grad_cols(at, span):
        p_all[:, pl.ds(at, span)] = jnp.dot(hid_t[...], scl[:, pl.ds(at, span)], preferred_element_type=F32).astype(BF16)

    def partial_ref(part, rz, rx):
        return p_all.at[shard_rows(rz, rx), cols[part]]

    def sum_task(part, rz, rx):
        kids = out_edges(part, rz, rx)
        total = partial_ref(part, rz, rx)[...].astype(F32)
        for d in kids:
            slot = SUM_SLOT[part, rz, rx, d]
            ref = sums[part].at[slot]
            remote(ref, ref, rs_s.at[0, 0], rs_r.at[which[part], slot], peer["zF"]).wait_recv()
            total = total + ref[...].astype(F32)
        if (rz, rx) != (0, 0):
            sums[part][SUM_SLOT[part, rz, rx, kids[0]]] = total.astype(BF16)
        elif part == "A":
            dg_ref[:, pl.ds(0, cut)] = total
            store_down_grad(0).start()
        else:
            dg_ref[:, pl.ds(cut, width - cut)] = total
            store_down_grad(1).start()

    def sum_push(part, rz, rx):
        kids = out_edges(part, rz, rx)
        src = sums[part].at[SUM_SLOT[part, rz, rx, kids[0]]] if kids else partial_ref(part, rz, rx)
        towards, slot = sum_target(part, rz, rx)
        push(src, sums[part].at[slot], rs_s.at[which[part], slot], rs_r.at[which[part], slot], peer[towards])

    def store_hidden_grad(i):
        at, span = backs[i]
        return pltpu.make_async_copy(hg.at[:, pl.ds(at, span)], hg_hbm.at[:, pl.ds(at, span)], hg_sem.at[i])

    def back_task(i):
        at, span = backs[i]
        prod = lax.dot_general(rows[...], w_all[pl.ds(at, span), :], (((1,), (1,)), ((), ())), preferred_element_type=F32)
        hg[:, pl.ds(at, span)] = (gate[:, 0:1] * prod).astype(BF16)
        weighted = hid[:, pl.ds(at, span)].astype(F32) * prod
        part = weighted[:, 0:LANES]
        for j in range(1, span // LANES):
            part = part + weighted[:, j * LANES:(j + 1) * LANES]
        sgrad[...] = part if i == 0 else sgrad[...] + part
        if i:
            store_hidden_grad(i - 1).start()
        if i == len(backs) - 1:
            store_hidden_grad(i).start()

    def give_task():
        for k in range(experts):
            s = lax.rem(exp + k, experts)
            total = jnp.sum(sgrad[pl.ds(pl.multiple_of(s * cap, cap), cap), :], axis=1, keepdims=True)
            row = jnp.sum(jnp.where(select_of(s), total, 0.0), axis=0, keepdims=True)
            if k == 0:
                ret_in[exp] = jnp.broadcast_to(row, (8, tokens))
            else:
                ret_out[k - 1] = jnp.broadcast_to(row, (8, tokens))
        for k in range(1, experts):
            push(ret_out.at[k - 1], ret_in.at[exp], ret_s.at[k - 1], ret_r.at[k - 1], others[k - 1])

    def logit_task():
        for k in range(1, experts):
            src = lax.rem(exp - k + experts, experts)
            remote(ret_in.at[src], ret_in.at[src], ret_s.at[0], ret_r.at[k - 1], others[0]).wait_recv()
        by_expert = jnp.concatenate([ret_in[e, 0:1, :] for e in range(experts)], axis=0)
        probs = gate_probs()
        grads = jnp.concatenate([jnp.sum(jnp.where(m, by_expert, 0.0), axis=0, keepdims=True) for m in matches()], axis=0)
        lo_ref[...] = probs * (grads - jnp.sum(probs * grads, axis=0, keepdims=True))

    emit = {
        "start": start, "meta": meta_task, "msend": meta_send, "mwait": meta_wait, "give": give_task, "logit": logit_task,
        "aw": gather_wait, "ap": gather_pass, "rs": sum_task, "rp": sum_push, "yp": y_push, "yw": y_wait, "sw": s_wait,
        "sel": sel_task, "pa": lambda i: grad_cols(*pa_cols[i]), "pb": lambda i: grad_cols(*pb_cols[i]),
        "turn": lambda i: turn_task(*turns[i]), "back": back_task,
    }
    for name in order:
        if name == ("turn", 0):
            loads["hid"].wait()
        emit[name[0]](*name[1:])
    for i in range(len(backs)):
        store_hidden_grad(i).wait()
    for i in (0, 1):
        store_down_grad(i).wait()
    for copy in sends:
        copy.wait_send()


def hand_on(parts, *refs):
    n = len(parts)
    srcs, dsts, bufs, (in_sem, out_sem) = refs[:n], refs[n:2 * n], refs[2 * n:3 * n], refs[3 * n:]
    pieces = [(a, pl.ds(i * size, size)) for a, (count, size) in enumerate(parts) for i in range(count)]
    loads = [pltpu.make_async_copy(srcs[a].at[at], bufs[a].at[at], in_sem.at[k]) for k, (a, at) in enumerate(pieces)]
    stores = [pltpu.make_async_copy(bufs[a].at[at], dsts[a].at[at], out_sem.at[k]) for k, (a, at) in enumerate(pieces)]
    for load in loads:
        load.start()
    for load, store in zip(loads, stores):
        load.wait()
        store.start()
    for store in stores:
        store.wait()


def handed_on(*arrays):
    parts = [(8, a.shape[0] // 8) if a.shape[0] >= 512 else (1, a.shape[0]) for a in arrays]
    total = sum(count for count, _ in parts)
    hbm = pl.BlockSpec(memory_space=pl.ANY)
    return pl.pallas_call(
        functools.partial(hand_on, parts),
        out_shape=tuple(jax.ShapeDtypeStruct(a.shape, a.dtype) for a in arrays),
        in_specs=[hbm] * len(arrays),
        out_specs=(hbm,) * len(arrays),
        scratch_shapes=[pltpu.VMEM(a.shape, a.dtype) for a in arrays]
        + [pltpu.SemaphoreType.DMA((total,)), pltpu.SemaphoreType.DMA((total,))],
    )(*arrays)


def per_device(grad_out, top_logits, expert_ids, saved_hidden, w_down):
    n_z, n_x, n_y = 8, 4, 4
    tokens, width = grad_out.shape
    hbm = pl.BlockSpec(memory_space=pl.ANY)
    slots, n_f = saved_hidden.shape[2:]
    shard = w_down.shape[1]
    top = top_logits.shape[1]
    experts = n_y * 2
    cap = slots // experts
    padded = width
    cut = padded * 2 // 5 // LANES * LANES

    def pieces(base, end, span=256):
        return [(at, min(span, end - at)) for at in range(base, end, span)]

    spans = (pieces(0, n_f), pieces(0, cut), pieces(cut, padded), pieces(0, n_f))
    tasks = task_list(*(len(p) for p in spans))
    order = [tasks[i] for i in ORDER]
    sizes = (n_z, n_x, n_y, tokens, width, padded, cut, shard, cap, top, experts, spans)
    vmem = pl.BlockSpec(memory_space=pltpu.VMEM)
    dma = pltpu.SemaphoreType.DMA
    logit, hidden_grad, down_grad = pl.pallas_call(
        functools.partial(body, sizes, order),
        out_shape=(
            jax.ShapeDtypeStruct((top, tokens), F32),
            jax.ShapeDtypeStruct((slots, n_f), BF16),
            jax.ShapeDtypeStruct((shard, width), F32),
        ),
        in_specs=[hbm, vmem, vmem, hbm, hbm],
        out_specs=(vmem, hbm, hbm),
        scratch_shapes=[
            pltpu.VMEM((n_f, padded), BF16),
            pltpu.VMEM((n_f, padded), BF16),
            pltpu.VMEM((experts, width, tokens), BF16),
            pltpu.VMEM((slots, padded), BF16),
            pltpu.VMEM((slots, padded), BF16),
            pltpu.VMEM((slots, n_f), BF16),
            pltpu.VMEM((n_f, slots), BF16),
            pltpu.VMEM((slots, n_f), BF16),
            pltpu.VMEM((N_EDGES, shard, cut), BF16),
            pltpu.VMEM((N_EDGES, shard, padded - cut), BF16),
            pltpu.VMEM((experts, 2 * experts, tokens), F32),
            pltpu.VMEM((experts, 8, tokens), F32),
            pltpu.VMEM((experts, 8, tokens), F32),
            pltpu.VMEM((slots, LANES), F32),
            pltpu.VMEM((slots, LANES), F32),
            pltpu.VMEM((width, tokens), BF16),
            pltpu.VMEM((shard, width), F32),
            dma((2, N_EDGES)), dma((2, len(NODES))),
            dma((2, N_EDGES)), dma((2, N_EDGES)),
            dma((3, 2)), dma((4, 2)), dma((4, 2)), dma((4, 2)),
            dma((experts - 1,)), dma((experts - 1,)), dma((experts - 1,)), dma((experts - 1,)), dma((3,)), dma((len(spans[3]),)), dma((2,)),
        ],
        compiler_params=pltpu.CompilerParams(collective_id=0, has_side_effects=True, vmem_limit_bytes=63000 * 1024),
    )(grad_out.T, top_logits.T, expert_ids.T, saved_hidden[0, 0], w_down[0])
    logit, hidden_grad, down_grad = handed_on(logit, hidden_grad, down_grad)
    return (logit.T, hidden_grad[None, None], down_grad[None])


def solution(mesh):
    return jax.shard_map(
        per_device,
        mesh=mesh,
        in_specs=(
            P(("ctx", "exp"), None),
            P(("ctx", "exp"), None),
            P(("ctx", "exp"), None),
            P("ctx", "exp", None, None),
            P("exp", "ctx", None),
        ),
        out_specs=(P(("ctx", "exp"), None), P("ctx", "exp", None, None), P("exp", "ctx", None)),
        check_vma=False,
    )
```

```python
import functools

import jax
import jax.numpy as jnp
from jax import lax
from jax.experimental import pallas as pl
from jax.experimental.pallas import tpu as pltpu
from jax.sharding import PartitionSpec as P

F32, BF16 = jnp.float32, jnp.bfloat16
LANES = 128
MESH = pl.DeviceIdType.MESH

RZ = (0, 1, -1, 2, -2, 3, -3, 4)
RX = (0, 1, -1, 2)


def out_edges(part, rz, rx):
    along_z, along_x = [], []
    if rz == 0:
        along_z = ["zF", "zR"]
    elif 0 < rz < 4:
        along_z = ["zF"]
    elif -3 < rz < 0:
        along_z = ["zR"]
    if rx == 0:
        along_x = ["xF", "xR"]
    elif rx == 1:
        along_x = ["xF"]
    if part == "A":
        return (along_x if rz == 0 else []) + along_z
    return (along_z if rx == 0 else []) + along_x


def parent_of(part, rz, rx):
    via_z = rz != 0 if part == "A" else rx == 0
    if via_z:
        return "zR" if rz > 0 else "zF"
    return "xR" if rx > 0 else "xF"


def moved(rz, rx, direction):
    step = 1 if direction[1] == "F" else -1
    return (rz + step, rx) if direction[0] == "z" else (rz, rx + step)


NODES = [(rz, rx) for rz in RZ for rx in RX]
SUM_SLOT = {}
SEND_ID = {}
for _part in "AB":
    _n = 0
    for _rz, _rx in NODES:
        for _d in out_edges(_part, _rz, _rx):
            SUM_SLOT[_part, _rz, _rx, _d] = _n
            SEND_ID[_part, _rz, _rx, _d] = _n
            _n += 1
N_EDGES = 31


def sum_target(part, rz, rx):
    towards = parent_of(part, rz, rx)
    back = towards[0] + ("R" if towards[1] == "F" else "F")
    step = -1 if back[1] == "F" else 1
    up = (rz + step, rx) if back[0] == "z" else (rz, rx + step)
    return towards, SUM_SLOT[part, *up, back]


def task_list(n_turn, n_pa, n_pb, n_back):
    out = [("start",), ("msend",), ("mwait",), ("give",), ("logit",)]
    for part in "AB":
        for rz, rx in NODES:
            if (rz, rx) != (0, 0):
                out.append(("aw", part, rz, rx))
            out += [("ap", part, rz, rx, d) for d in out_edges(part, rz, rx)]
    for part in "AB":
        for rz, rx in NODES:
            if out_edges(part, rz, rx):
                out.append(("rs", part, rz, rx))
            if (rz, rx) != (0, 0):
                out.append(("rp", part, rz, rx))
    for h in (0, 1):
        out += [("yp", 0, h, "yF"), ("yp", 0, h, "yR"), ("yp", 0, h, "ss")]
        for ry in (1, -1, 2):
            out.append(("yw", ry, h))
            out.append(("yp", ry, h, "ss"))
        out.append(("yp", 1, h, "yF"))
        out += [("sw", ry, h) for ry in (0, 1, -1, 2)]
    for own in (1, 0):
        out += [("sel", own, ry) for ry in (0, 1, -1, 2)]
    out += [("turn", i) for i in range(n_turn)]
    out += [("pa", i) for i in range(n_pa)]
    out += [("pb", i) for i in range(n_pb)]
    out += [("back", i) for i in range(n_back)]
    return out


ORDER = [
    0, 5, 68, 6, 67, 1, 233, 231, 70, 69, 232, 7, 246, 245, 259, 247, 241, 8, 9, 10, 11, 13, 14, 255,
    15, 83, 85, 86, 75, 76, 77, 78, 84, 71, 72, 27, 73, 19, 20, 16, 17, 31, 21, 22, 234, 240, 235, 236,
    237, 32, 89, 23, 242, 87, 88, 24, 99, 101, 100, 102, 243, 81, 47, 91, 92, 79, 94, 93, 48, 35, 36, 248,
    254, 249, 267, 268, 269, 270, 271, 272, 2, 263, 260, 250, 251, 261, 74, 18, 115, 105, 117, 25, 256, 26, 264, 80,
    257, 265, 12, 61, 238, 239, 37, 38, 90, 97, 116, 28, 33, 244, 39, 252, 253, 40, 262, 34, 103, 104, 29, 120,
    258, 266, 273, 107, 95, 96, 43, 108, 110, 30, 274, 109, 275, 82, 51, 52, 276, 49, 277, 183, 176, 278, 118, 41,
    279, 119, 280, 45, 281, 53, 181, 42, 282, 113, 106, 283, 284, 55, 174, 224, 223, 229, 175, 56, 230, 218, 98, 111,
    180, 54, 170, 122, 123, 124, 46, 178, 158, 63, 121, 221, 112, 159, 179, 222, 168, 160, 169, 161, 60, 57, 227, 211,
    228, 171, 58, 142, 65, 215, 193, 143, 177, 152, 64, 212, 125, 153, 154, 164, 127, 165, 126, 194, 155, 166, 167, 114,
    219, 220, 44, 205, 144, 136, 216, 145, 50, 66, 138, 225, 217, 206, 226, 162, 59, 163, 209, 148, 62, 149, 187, 200,
    139, 150, 128, 285, 191, 151, 182, 210, 286, 287, 137, 288, 289, 172, 146, 213, 203, 173, 147, 204, 290, 134, 197, 135,
    198, 214, 3, 188, 199, 207, 208, 192, 156, 157, 201, 202, 130, 131, 140, 141, 195, 196, 185, 186, 189, 190, 132, 133,
    4, 129, 184,
]


def body(sizes, order, *refs):
    (n_z, n_x, n_y, tokens, width, padded, cut, shard, cap, top, experts, spans) = sizes
    turns, pa_cols, pb_cols, backs = spans
    (go_hbm, lg_ref, ids_ref, hid_hbm, w_hbm, lo_ref, hg_hbm, dg_hbm,
     w_all, p_all, tok, rows, scl, hid, hid_t, hg, sum_a, sum_b, meta, ret_in, ret_out, gate, sgrad, go_ref, dg_ref,
     ag_s, ag_r, rs_s, rs_r, y_s, y_r, sib_s, sib_r, meta_s, meta_r, ret_s, ret_r, in_sem, hg_sem, dg_sem) = refs
    ctx, exp = lax.axis_index("ctx"), lax.axis_index("exp")
    z, x, y, core = ctx // n_x, ctx % n_x, exp // 2, exp % 2
    sense = 1 - 2 * core
    half = width // 2

    def ctx_dev(zz, xx):
        return (lax.rem(zz + 2 * n_z, n_z) * n_x + lax.rem(xx + 2 * n_x, n_x), exp)

    def exp_dev(yy, cc):
        return (ctx, lax.rem(yy + 2 * n_y, n_y) * 2 + cc)

    peer = {
        "zF": ctx_dev(z + sense, x), "zR": ctx_dev(z - sense, x),
        "xF": ctx_dev(z, x + sense), "xR": ctx_dev(z, x - sense),
        "yF": exp_dev(y + sense, core), "yR": exp_dev(y - sense, core),
        "ss": exp_dev(y, 1 - core),
    }
    others = [(ctx, lax.rem(exp + k, experts)) for k in range(1, experts)]
    slots = experts * cap
    barrier = pltpu.get_barrier_semaphore()
    greeted = [peer["zF"], peer["zR"], peer["xF"], peer["xR"]] + others
    for dev in greeted:
        pl.semaphore_signal(barrier, inc=1, device_id=dev, device_id_type=MESH)

    def shard_rows(rz, rx):
        zz = lax.rem(z - sense * rz + 2 * n_z, n_z)
        xx = lax.rem(x - sense * rx + 2 * n_x, n_x)
        return pl.ds(pl.multiple_of((zz * n_x + xx) * shard, shard), shard)

    cols = {"A": pl.ds(0, cut), "B": pl.ds(cut, padded - cut)}
    sums = {"A": sum_a, "B": sum_b}
    which = {"A": 0, "B": 1}
    sends = []

    def remote(src, dst, s_sem, r_sem, dev):
        return pltpu.make_async_remote_copy(
            src_ref=src, dst_ref=dst, send_sem=s_sem, recv_sem=r_sem, device_id=dev, device_id_type=MESH
        )

    def push(*args):
        copy = remote(*args)
        copy.start()
        sends.append(copy)

    def gather_recv_sem(part, rz, rx):
        return ag_r.at[which[part], NODES.index((rz, rx))]

    def gather_pass(part, rz, rx, d):
        ref = w_all.at[shard_rows(rz, rx), cols[part]]
        src = w_hbm.at[:, cols[part]] if (rz, rx) == (0, 0) else ref
        push(src, ref, ag_s.at[which[part], SEND_ID[part, rz, rx, d]], gather_recv_sem(part, *moved(rz, rx, d)), peer[d])

    def gather_wait(part, rz, rx):
        ref = w_all.at[shard_rows(rz, rx), cols[part]]
        remote(ref, ref, ag_s.at[0, 0], gather_recv_sem(part, rz, rx), peer["zF"]).wait_recv()

    Y_INDEX = {0: 0, 1: 1, -1: 2, 2: 3}

    def block_of(own, ry):
        yy = lax.rem(y - sense * ry + 2 * n_y, n_y) if own else lax.rem(y + sense * ry + 2 * n_y, n_y)
        return yy * 2 + (core if own else 1 - core)

    def half_ref(own, ry, h):
        return tok.at[block_of(own, ry), pl.ds(h * half, half)]

    def y_push(ry, h, d):
        ref = half_ref(True, ry, h)
        src = go_hbm.at[pl.ds(h * half, half)] if ry == 0 else ref
        if d == "ss":
            push(src, ref, sib_s.at[Y_INDEX[ry], h], sib_r.at[Y_INDEX[ry], h], peer["ss"])
            return
        to = ry + (1 if d == "yF" else -1)
        push(src, ref, y_s.at[{"yF": ry, "yR": 2}[d], h], y_r.at[Y_INDEX[to], h], peer[d])

    def y_wait(ry, h):
        ref = half_ref(True, ry, h)
        remote(ref, ref, y_s.at[0, 0], y_r.at[Y_INDEX[ry], h], peer["yF"]).wait_recv()

    def s_wait(ry, h):
        ref = half_ref(False, ry, h)
        remote(ref, ref, y_s.at[0, 0], sib_r.at[Y_INDEX[ry], h], peer["ss"]).wait_recv()

    loads = {
        "w": pltpu.make_async_copy(w_hbm, w_all.at[shard_rows(0, 0)], in_sem.at[0]),
        "go": pltpu.make_async_copy(go_hbm, go_ref, in_sem.at[1]),
        "hid": pltpu.make_async_copy(hid_hbm, hid, in_sem.at[2]),
    }

    def start():
        for name in ("w", "go", "hid"):
            loads[name].start()
        meta_task()
        pl.semaphore_wait(barrier, len(greeted))

    def store_down_grad(i):
        at = (pl.ds(0, cut), pl.ds(cut, width - cut))[i]
        return pltpu.make_async_copy(dg_ref.at[:, at], dg_hbm.at[:, at], dg_sem.at[i])

    def gate_probs():
        logits = lg_ref[...]
        weights = jnp.exp(logits - jnp.max(logits, axis=0, keepdims=True))
        return weights / jnp.sum(weights, axis=0, keepdims=True)

    def matches():
        row = lax.broadcasted_iota(jnp.int32, (experts, tokens), 0)
        ids = ids_ref[...]
        return [ids[k:k + 1, :] == row for k in range(top)]

    def meta_task():
        sent = gate_probs().astype(BF16).astype(F32)
        chosen = jnp.zeros((experts, tokens), F32)
        by_expert = jnp.zeros((experts, tokens), F32)
        for k, match in enumerate(matches()):
            chosen = chosen + jnp.where(match, 1.0, 0.0)
            by_expert = by_expert + jnp.where(match, sent[k:k + 1, :], 0.0)
        earlier = lax.broadcasted_iota(jnp.int32, (tokens, tokens), 0) < lax.broadcasted_iota(jnp.int32, (tokens, tokens), 1)
        rank = jnp.dot(chosen.astype(BF16), jnp.where(earlier, 1.0, 0.0).astype(BF16), preferred_element_type=F32)
        meta[exp, pl.ds(0, experts), :] = jnp.where(chosen > 0.5, rank, -1.0)
        meta[exp, pl.ds(experts, experts), :] = by_expert

    def meta_send():
        for k in range(1, experts):
            push(meta.at[exp], meta.at[exp], meta_s.at[k - 1], meta_r.at[k - 1], others[k - 1])

    def meta_wait():
        for k in range(1, experts):
            src = lax.rem(exp - k + experts, experts)
            remote(meta.at[src], meta.at[src], meta_s.at[0], meta_r.at[k - 1], others[0]).wait_recv()

    def select_of(s):
        rank = meta[s, pl.ds(exp, 1), :]
        slot = lax.broadcasted_iota(jnp.int32, (cap, tokens), 0).astype(F32)
        return rank == slot

    def sel_task(own, ry):
        s = block_of(own, ry)
        select = select_of(s)
        gates = jnp.sum(jnp.where(select, meta[s, pl.ds(experts + exp, 1), :], 0.0), axis=1, keepdims=True)
        at = pl.ds(pl.multiple_of(s * cap, cap), cap)
        gate[at, :] = jnp.broadcast_to(gates, (cap, LANES))
        block = go_ref[...] if own and ry == 0 else tok[s]
        picked = lax.dot_general(
            jnp.where(select, 1.0, 0.0).astype(BF16), block, (((1,), (1,)), ((), ())), preferred_element_type=F32
        )
        rows[at, pl.ds(0, width)] = picked.astype(BF16)
        scl[at, pl.ds(0, width)] = (gates * picked).astype(BF16)

    def turn_task(at, span):
        hid_t[pl.ds(at, span), :] = hid[:, pl.ds(at, span)].T

    def grad_cols(at, span):
        p_all[:, pl.ds(at, span)] = jnp.dot(hid_t[...], scl[:, pl.ds(at, span)], preferred_element_type=F32).astype(BF16)

    def partial_ref(part, rz, rx):
        return p_all.at[shard_rows(rz, rx), cols[part]]

    def sum_task(part, rz, rx):
        kids = out_edges(part, rz, rx)
        total = partial_ref(part, rz, rx)[...].astype(F32)
        for d in kids:
            slot = SUM_SLOT[part, rz, rx, d]
            ref = sums[part].at[slot]
            remote(ref, ref, rs_s.at[0, 0], rs_r.at[which[part], slot], peer["zF"]).wait_recv()
            total = total + ref[...].astype(F32)
        if (rz, rx) != (0, 0):
            sums[part][SUM_SLOT[part, rz, rx, kids[0]]] = total.astype(BF16)
        elif part == "A":
            dg_ref[:, pl.ds(0, cut)] = total
            store_down_grad(0).start()
        else:
            dg_ref[:, pl.ds(cut, width - cut)] = total
            store_down_grad(1).start()

    def sum_push(part, rz, rx):
        kids = out_edges(part, rz, rx)
        src = sums[part].at[SUM_SLOT[part, rz, rx, kids[0]]] if kids else partial_ref(part, rz, rx)
        towards, slot = sum_target(part, rz, rx)
        push(src, sums[part].at[slot], rs_s.at[which[part], slot], rs_r.at[which[part], slot], peer[towards])

    def store_hidden_grad(i):
        at, span = backs[i]
        return pltpu.make_async_copy(hg.at[:, pl.ds(at, span)], hg_hbm.at[:, pl.ds(at, span)], hg_sem.at[i])

    def back_task(i):
        at, span = backs[i]
        prod = lax.dot_general(rows[...], w_all[pl.ds(at, span), :], (((1,), (1,)), ((), ())), preferred_element_type=F32)
        hg[:, pl.ds(at, span)] = (gate[:, 0:1] * prod).astype(BF16)
        weighted = hid[:, pl.ds(at, span)].astype(F32) * prod
        part = weighted[:, 0:LANES]
        for j in range(1, span // LANES):
            part = part + weighted[:, j * LANES:(j + 1) * LANES]
        sgrad[...] = part if i == 0 else sgrad[...] + part
        if i:
            store_hidden_grad(i - 1).start()
        if i == len(backs) - 1:
            store_hidden_grad(i).start()

    def give_task():
        for k in range(experts):
            s = lax.rem(exp + k, experts)
            total = jnp.sum(sgrad[pl.ds(pl.multiple_of(s * cap, cap), cap), :], axis=1, keepdims=True)
            row = jnp.sum(jnp.where(select_of(s), total, 0.0), axis=0, keepdims=True)
            if k == 0:
                ret_in[exp] = jnp.broadcast_to(row, (8, tokens))
            else:
                ret_out[k - 1] = jnp.broadcast_to(row, (8, tokens))
        for k in range(1, experts):
            push(ret_out.at[k - 1], ret_in.at[exp], ret_s.at[k - 1], ret_r.at[k - 1], others[k - 1])

    def logit_task():
        for k in range(1, experts):
            src = lax.rem(exp - k + experts, experts)
            remote(ret_in.at[src], ret_in.at[src], ret_s.at[0], ret_r.at[k - 1], others[0]).wait_recv()
        by_expert = jnp.concatenate([ret_in[e, 0:1, :] for e in range(experts)], axis=0)
        probs = gate_probs()
        grads = jnp.concatenate([jnp.sum(jnp.where(m, by_expert, 0.0), axis=0, keepdims=True) for m in matches()], axis=0)
        lo_ref[...] = probs * (grads - jnp.sum(probs * grads, axis=0, keepdims=True))

    emit = {
        "start": start, "msend": meta_send, "mwait": meta_wait, "give": give_task, "logit": logit_task,
        "aw": gather_wait, "ap": gather_pass, "rs": sum_task, "rp": sum_push, "yp": y_push, "yw": y_wait, "sw": s_wait,
        "sel": sel_task, "pa": lambda i: grad_cols(*pa_cols[i]), "pb": lambda i: grad_cols(*pb_cols[i]),
        "turn": lambda i: turn_task(*turns[i]), "back": back_task,
    }
    for name in order:
        if name == ("turn", 0):
            loads["hid"].wait()
        if name == ("sel", 1, 0):
            loads["go"].wait()
        if name == ("back", 0):
            loads["w"].wait()
        emit[name[0]](*name[1:])
    for i in range(len(backs)):
        store_hidden_grad(i).wait()
    for i in (0, 1):
        store_down_grad(i).wait()
    for copy in sends:
        copy.wait_send()


def hand_on(parts, *refs):
    n = len(parts)
    srcs, dsts, bufs, (in_sem, out_sem) = refs[:n], refs[n:2 * n], refs[2 * n:3 * n], refs[3 * n:]
    pieces = [(a, pl.ds(i * size, size)) for a, (count, size) in enumerate(parts) for i in range(count)]
    loads = [pltpu.make_async_copy(srcs[a].at[at], bufs[a].at[at], in_sem.at[k]) for k, (a, at) in enumerate(pieces)]
    stores = [pltpu.make_async_copy(bufs[a].at[at], dsts[a].at[at], out_sem.at[k]) for k, (a, at) in enumerate(pieces)]
    for load in loads:
        load.start()
    for load, store in zip(loads, stores):
        load.wait()
        store.start()
    for store in stores:
        store.wait()


def handed_on(*arrays):
    parts = [(8, a.shape[0] // 8) if a.shape[0] >= 512 else (1, a.shape[0]) for a in arrays]
    total = sum(count for count, _ in parts)
    hbm = pl.BlockSpec(memory_space=pl.ANY)
    return pl.pallas_call(
        functools.partial(hand_on, parts),
        out_shape=tuple(jax.ShapeDtypeStruct(a.shape, a.dtype) for a in arrays),
        in_specs=[hbm] * len(arrays),
        out_specs=(hbm,) * len(arrays),
        scratch_shapes=[pltpu.VMEM(a.shape, a.dtype) for a in arrays]
        + [pltpu.SemaphoreType.DMA((total,)), pltpu.SemaphoreType.DMA((total,))],
    )(*arrays)


def per_device(grad_out, top_logits, expert_ids, saved_hidden, w_down):
    n_z, n_x, n_y = 8, 4, 4
    tokens, width = grad_out.shape
    hbm = pl.BlockSpec(memory_space=pl.ANY)
    slots, n_f = saved_hidden.shape[2:]
    shard = w_down.shape[1]
    top = top_logits.shape[1]
    experts = n_y * 2
    cap = slots // experts
    padded = width
    cut = padded * 2 // 5 // LANES * LANES

    def pieces(base, end, span=256):
        return [(at, min(span, end - at)) for at in range(base, end, span)]

    spans = (pieces(0, n_f), pieces(0, cut), pieces(cut, padded), pieces(0, n_f))
    tasks = task_list(*(len(p) for p in spans))
    order = [tasks[i] for i in ORDER]
    sizes = (n_z, n_x, n_y, tokens, width, padded, cut, shard, cap, top, experts, spans)
    vmem = pl.BlockSpec(memory_space=pltpu.VMEM)
    dma = pltpu.SemaphoreType.DMA
    logit, hidden_grad, down_grad = pl.pallas_call(
        functools.partial(body, sizes, order),
        out_shape=(
            jax.ShapeDtypeStruct((top, tokens), F32),
            jax.ShapeDtypeStruct((slots, n_f), BF16),
            jax.ShapeDtypeStruct((shard, width), F32),
        ),
        in_specs=[hbm, vmem, vmem, hbm, hbm],
        out_specs=(vmem, hbm, hbm),
        scratch_shapes=[
            pltpu.VMEM((n_f, padded), BF16),
            pltpu.VMEM((n_f, padded), BF16),
            pltpu.VMEM((experts, width, tokens), BF16),
            pltpu.VMEM((slots, padded), BF16),
            pltpu.VMEM((slots, padded), BF16),
            pltpu.VMEM((slots, n_f), BF16),
            pltpu.VMEM((n_f, slots), BF16),
            pltpu.VMEM((slots, n_f), BF16),
            pltpu.VMEM((N_EDGES, shard, cut), BF16),
            pltpu.VMEM((N_EDGES, shard, padded - cut), BF16),
            pltpu.VMEM((experts, 2 * experts, tokens), F32),
            pltpu.VMEM((experts, 8, tokens), F32),
            pltpu.VMEM((experts, 8, tokens), F32),
            pltpu.VMEM((slots, LANES), F32),
            pltpu.VMEM((slots, LANES), F32),
            pltpu.VMEM((width, tokens), BF16),
            pltpu.VMEM((shard, width), F32),
            dma((2, N_EDGES)), dma((2, len(NODES))),
            dma((2, N_EDGES)), dma((2, N_EDGES)),
            dma((3, 2)), dma((4, 2)), dma((4, 2)), dma((4, 2)),
            dma((experts - 1,)), dma((experts - 1,)), dma((experts - 1,)), dma((experts - 1,)), dma((3,)), dma((len(spans[3]),)), dma((2,)),
        ],
        compiler_params=pltpu.CompilerParams(collective_id=0, has_side_effects=True, vmem_limit_bytes=63000 * 1024),
    )(grad_out.T, top_logits.T, expert_ids.T, saved_hidden[0, 0], w_down[0])
    logit, hidden_grad, down_grad = handed_on(logit, hidden_grad, down_grad)
    return (logit.T, hidden_grad[None, None], down_grad[None])


def solution(mesh):
    return jax.shard_map(
        per_device,
        mesh=mesh,
        in_specs=(
            P(("ctx", "exp"), None),
            P(("ctx", "exp"), None),
            P(("ctx", "exp"), None),
            P("ctx", "exp", None, None),
            P("exp", "ctx", None),
        ),
        out_specs=(P(("ctx", "exp"), None), P("ctx", "exp", None, None), P("exp", "ctx", None)),
        check_vma=False,
    )
```
